512 devices in a mesh: rows: 64 (over y, x, core), sub: 8 (over z).
Axes of the slice: x: 4, y: 8, z: 8, core: 2. Of those that a mesh axis runs over, the one named last changes fastest.
Arguments:
- stiffness: bfloat16 [16384, 64, 512], P(('rows', 'sub')), may hold values from -0.75 to 0.75
- prolongator: bfloat16 [16384, 64, 64], P(('rows', 'sub')), may hold values from -0.75 to 0.75
- column_index: int32 [16384, 8], P(('rows', 'sub')), may hold values from 0 to 16383, as said below
- slot_index: int32 [16384, 8], P(('rows', 'sub')), may hold values from 0 to 64, as said below
- place_index: int32 [512, 64], P(('rows', 'sub')), may hold values from 0 to 63, as said below
Outputs:
- coarse: float32 [4096, 64, 64], P(('rows', 'sub'))
The draws below stay inside these ranges and needn't reach their ends.
Inputs may be any that keep to these rules, and one draw needn't show every extreme that they name: column_index[i, 0] = i, and every column lies within 4 rows of the 32 rows of the device that holds row i. `slot_index`: in each row the empty blocks come last, and at least half of a row's blocks are not empty. For each slot j and each s below 8, the devices d with d % 8 == s give place_index[d, j] // 8 each value from 0 to 7 exactly 64 // 8 times.
All inputs are finite; a program needn't handle non-finite values.
Results may differ from the reference program's by a relative error of at most 0.0029.
Values may be sent and summed in bfloat16 or wider, within the bound.
No kernel may reach another device: no remote copies, remote signals or barrier semaphores. Data moves between devices by JAX's collectives and lax.ppermute only.
A program may use at most 64 MiB of HBM per device.

```python
import jax
import jax.numpy as jnp
from jax import lax

BLOCK = 64
BLOCKS_ROW = 8
ROWS_DEV = 32
COARSE_DEV = 8
REACH = 4
ROW_TABLE = 64
FINE_ROWS = 16384
COARSE_ALL = 4096
N_ROWS = 64
N_SUB = 8
DEVICES = 512


def draw_column_index(key, part):
    rows_all = jnp.arange(FINE_ROWS, dtype=jnp.int32)[:, None]
    start = rows_all // ROWS_DEV * ROWS_DEV
    offset = jax.random.randint(key, (FINE_ROWS, BLOCKS_ROW), 0, ROWS_DEV + 2 * REACH, dtype=jnp.int32)
    column = jnp.clip(start - REACH + offset, 0, FINE_ROWS - 1)
    position = jnp.arange(BLOCKS_ROW, dtype=jnp.int32)[None, :]
    return jnp.where(position == 0, rows_all, column).astype(jnp.int32)


def draw_slot_index(key, part):
    first_key, second_key = jax.random.split(jax.random.fold_in(key, 11))
    live = jax.random.randint(first_key, (FINE_ROWS, 1), BLOCKS_ROW // 2, BLOCKS_ROW + 1, dtype=jnp.int32)
    live = live.at[0, 0].set(BLOCKS_ROW // 2)
    slots = jax.random.randint(second_key, (FINE_ROWS, BLOCKS_ROW), 0, N_ROWS, dtype=jnp.int32)
    slots = slots.at[0, 0].set(0)
    position = jnp.arange(BLOCKS_ROW, dtype=jnp.int32)[None, :]
    return jnp.where(position < live, slots, N_ROWS).astype(jnp.int32)


def draw_place_index(key, part):
    first_key, second_key = jax.random.split(jax.random.fold_in(key, 23))
    scores = jax.random.randint(first_key, (N_SUB, N_ROWS, N_ROWS), 0, 65536, dtype=jnp.int32) * N_ROWS
    scores = scores + jnp.arange(N_ROWS, dtype=jnp.int32)[None, None, :]
    order = jnp.argsort(scores, axis=-1).astype(jnp.int32)
    group = order % N_SUB
    offset = jax.random.randint(second_key, (N_SUB, N_ROWS, N_ROWS), 0, COARSE_DEV, dtype=jnp.int32)
    slot_ids = jnp.arange(N_ROWS, dtype=jnp.int32)[None, :, None]
    offset = jnp.where(slot_ids == 0, 0, offset)
    offset = jnp.where(slot_ids == N_ROWS - 1, COARSE_DEV - 1, offset)
    places = group * COARSE_DEV + offset
    places = jnp.transpose(places, (2, 0, 1)).reshape(DEVICES, N_ROWS)
    return places.astype(jnp.int32)


def levels(rng, dims, cuts, low, top_value):
    gain = 1.0
    for dim, shards_of in cuts:
        draws = jax.random.uniform(jax.random.fold_in(jax.random.fold_in(rng, 6), dim), (shards_of,), jnp.float32, low / len(cuts), top_value / len(cuts))
        gain = gain * jnp.repeat(jnp.exp(draws), dims[dim] // shards_of).reshape((-1,) + (1,) * (len(dims) - 1 - dim))
    return gain


def centred(rng, shape, spread, limit, cuts=(), kind=jnp.bfloat16):
    array = jax.random.normal(rng, shape, jnp.float32) * spread
    if len(cuts) > 0:
        array = levels(rng, shape, cuts, -0.22, 0.18) * array
    return jnp.clip(array, min=-limit, max=limit).astype(kind)


def setup_inputs(seed: int = 0) -> dict:
    key_of = jax.random.split(jax.random.key(seed), 6)
    return {
        "stiffness": centred(key_of[0], (FINE_ROWS, BLOCK, BLOCKS_ROW * BLOCK), BLOCK ** -0.5, 0.75, ((0, 512),)),
        "prolongator": centred(key_of[1], (FINE_ROWS, BLOCK, BLOCK), BLOCK ** -0.5, 0.75, ((0, 512),)),
        "column_index": draw_column_index(jax.random.fold_in(key_of[5], 71), 0),
        "slot_index": draw_slot_index(jax.random.fold_in(key_of[5], 71), 0),
        "place_index": draw_place_index(jax.random.fold_in(key_of[5], 71), 0),
    }


def reference(stiffness, prolongator, column_index, slot_index, place_index):
    def one_device(table, device):
        first = device * ROWS_DEV
        rows_a = lax.dynamic_slice_in_dim(stiffness, first, ROWS_DEV, 0).reshape(ROWS_DEV, BLOCK, BLOCKS_ROW, BLOCK)
        own = lax.dynamic_slice_in_dim(prolongator, first, ROWS_DEV, 0)
        columns = lax.dynamic_slice_in_dim(column_index, first, ROWS_DEV, 0)
        slots = lax.dynamic_slice_in_dim(slot_index, first, ROWS_DEV, 0)
        places = lax.dynamic_slice_in_dim(place_index, device, 1, 0)[0]
        neighbour = prolongator[columns]
        middle = jnp.einsum("rakb,rkbc->rakc", rows_a.astype(jnp.float32), neighbour.astype(jnp.float32)).astype(jnp.bfloat16)
        terms = jnp.einsum("rba,rbkc->rkac", own.astype(jnp.float32), middle.astype(jnp.float32))
        live = slots < N_ROWS
        safe = jnp.minimum(slots, N_ROWS - 1)
        target = (safe * ROW_TABLE + places[safe]).astype(jnp.int32)
        terms = jnp.where(live[:, :, None, None], terms, jnp.zeros_like(terms))
        table = table.at[target.reshape(-1)].add(terms.reshape(-1, BLOCK, BLOCK))
        return table, None

    table = jnp.zeros((COARSE_ALL, BLOCK, BLOCK), jnp.float32)
    table, unused = lax.scan(one_device, table, jnp.arange(DEVICES, dtype=jnp.int32))
    return table
```

```python
import jax
import jax.numpy as jnp
from jax import lax
from jax.experimental import pallas as pl
from jax.experimental.pallas import tpu as pltpu
from jax.sharding import PartitionSpec as P

COARSE_DEV = 8
REACH = 4
LANES = 128
STEPS = 4
NOTE = 8


def product_kernel(cols, slots, places, a_ref, own_ref, low_ref, high_ref, out_ref, left, right, own_t, even, odd):
    step = pl.program_id(0)
    owners, packed, _ = out_ref.shape
    half = (packed - NOTE)
    width = own_ref.shape[1]
    rows_own = own_ref.shape[0]
    rows_step, stored = a_ref.shape[0], cols.shape[0]

    @pl.when(step == 0)
    def _():
        zero = jnp.zeros((width, width), own_ref.dtype)

        def place(index, block):
            left[index] = jnp.concatenate([block, zero], axis=1)
            right[index] = jnp.concatenate([zero, block], axis=1)

        for n in range(REACH):
            place(n, low_ref[n])
            place(REACH + rows_own + n, high_ref[n])

        @pl.loop(0, rows_own)
        def _(n):
            block = own_ref[n]
            place(REACH + n, block)
            own_t[n] = block.T

        @pl.loop(0, even.shape[0])
        def _(n):
            even[n] = jnp.zeros(even.shape[1:], even.dtype)
            odd[n] = jnp.zeros(odd.shape[1:], odd.dtype)

    base = cols[0, 0] - REACH

    @pl.loop(0, rows_step)
    def _(n):
        row = step * rows_step + n
        middles = []
        for k in range(0, stored, 2):
            sides = jnp.concatenate([left[cols[k, row] - base], right[cols[k + 1, row] - base]], axis=0)
            pair = jnp.dot(a_ref[n, :, k * width:(k + 2) * width], sides, preferred_element_type=jnp.float32)
            middles.append(pair.astype(jnp.bfloat16))
        terms = jnp.dot(own_t[row], jnp.concatenate(middles, axis=1), preferred_element_type=jnp.float32)
        for k in range(0, stored, 2):
            pair = terms[:, k * width:(k + 2) * width]
            even[slots[k, row]] += pair
            odd[slots[k + 1, row]] += pair

    @pl.when(step == pl.num_programs(0) - 1)
    def _():
        lane = lax.broadcasted_iota(jnp.int32, (half, LANES), 1)

        @pl.loop(0, owners)
        def _(j):
            e, o = even[j], odd[j]
            top = e[:half] + pltpu.roll(o[:half], width, 1)
            low = pltpu.roll(e[half:], width, 1) + o[half:]
            out_ref[j, :half] = jnp.where(lane < width, top, low).astype(out_ref.dtype)
            out_ref[j, half:] = jnp.full((NOTE, LANES), places[0, j].astype(jnp.float32), jnp.float32).astype(out_ref.dtype)


def route_kernel(in_ref, out_ref, count):
    blocks, packed, _ = in_ref.shape
    half = packed - NOTE
    groups = out_ref.shape[0]
    each = blocks // groups
    for g in range(groups):
        count[g] = 0
    for n in range(blocks):
        place = in_ref[n, half:].astype(jnp.float32)[0, 0].astype(jnp.int32)
        g = place // COARSE_DEV
        rank = count[g]
        count[g] = rank + 1
        out_ref[g, rank] = in_ref[n]


def sum_kernel(in_ref, out_ref, total):
    groups, each, packed, _ = in_ref.shape
    half = packed - NOTE
    width = out_ref.shape[2]
    total[...] = jnp.zeros_like(total)
    for g in range(groups):
        for n in range(each):
            place = in_ref[g, n, half:].astype(jnp.float32)[0, 0].astype(jnp.int32)
            total[place % COARSE_DEV] += in_ref[g, n, :half].astype(jnp.float32)
    for n in range(out_ref.shape[0]):
        block = total[n]
        out_ref[n, :half] = block[:, :width]
        out_ref[n, half:] = block[:, width:]


def body(stiffness, prolongator, column_index, slot_index, place_index):
    row_count, width, _ = prolongator.shape
    stored = column_index.shape[1]
    owners, groups = lax.axis_size("rows"), lax.axis_size("sub")
    axes = ("rows", "sub")
    count = owners * groups
    up = [(i, i + 1) for i in range(count - 1)]
    low = lax.ppermute(prolongator[row_count - REACH:], axes, up)
    high = lax.ppermute(prolongator[:REACH], axes, [(b, a) for a, b in up])
    half = width * width // LANES
    packed = half + NOTE
    smem = pl.BlockSpec(memory_space=pltpu.SMEM)
    vmem = pl.BlockSpec(memory_space=pltpu.VMEM)
    rows_step = row_count // STEPS
    sent = pl.pallas_call(
        product_kernel,
        grid=(STEPS,),
        out_shape=jax.ShapeDtypeStruct((owners, packed, LANES), jnp.bfloat16),
        in_specs=[smem, smem, smem, pl.BlockSpec((rows_step, width, stored * width), lambda n: (n, 0, 0)), vmem, vmem, vmem],
        out_specs=vmem,
        scratch_shapes=[
            pltpu.VMEM((row_count + 2 * REACH, width, LANES), jnp.bfloat16),
            pltpu.VMEM((row_count + 2 * REACH, width, LANES), jnp.bfloat16),
            pltpu.VMEM((row_count, width, width), jnp.bfloat16),
            pltpu.VMEM((owners + 1, width, LANES), jnp.float32),
            pltpu.VMEM((owners + 1, width, LANES), jnp.float32),
        ],
        name="product",
    )(column_index.T, slot_index.T, place_index, stiffness, prolongator, low, high)
    received = lax.all_to_all(sent, "rows", 0, 0, tiled=True)
    routed = pl.pallas_call(
        route_kernel,
        out_shape=jax.ShapeDtypeStruct((groups, owners // groups, packed, LANES), jnp.bfloat16),
        in_specs=[vmem],
        out_specs=vmem,
        scratch_shapes=[pltpu.SMEM((groups,), jnp.int32)],
        name="route",
    )(received)
    gathered = lax.all_to_all(routed, "sub", 0, 0, tiled=True)
    return pl.pallas_call(
        sum_kernel,
        out_shape=jax.ShapeDtypeStruct((COARSE_DEV, width, width), jnp.float32),
        in_specs=[vmem],
        out_specs=vmem,
        scratch_shapes=[pltpu.VMEM((COARSE_DEV, half, LANES), jnp.float32)],
        name="total",
    )(gathered)


def solution(mesh):
    split = ("rows", "sub")
    in_specs = (P(split, None, None), P(split, None, None), P(split, None), P(split, None), P(split, None))
    return jax.shard_map(body, mesh=mesh, in_specs=in_specs, out_specs=P(split, None, None), check_vma=False)
```

```python
import jax
import jax.numpy as jnp
from jax import lax
from jax.experimental import pallas as pl
from jax.experimental.pallas import tpu as pltpu
from jax.sharding import PartitionSpec as P

COARSE_DEV = 8
REACH = 4
LANES = 128
BATCH = 16
VMEM_PRODUCT = 60 << 20
VMEM_SMALL = 8 << 20
STEPS = 2
NOTE = 8


def product_kernel(cols, slots, places, a_ref, own_ref, first_ref, second_ref, out_ref, left, right, own_t, even, odd):
    step = pl.program_id(0)
    owners, packed, _ = out_ref.shape
    half = (packed - NOTE)
    width = own_ref.shape[1]
    rows_own = own_ref.shape[0]
    rows_step, stored = a_ref.shape[0], cols.shape[0]

    @pl.when(step == 0)
    def _():
        zero = jnp.zeros((width, width), own_ref.dtype)

        def place(index, block):
            left[index] = jnp.concatenate([block, zero], axis=1)
            right[index] = jnp.concatenate([zero, block], axis=1)

        odd_device = (cols[0, 0] // rows_own) % 2
        above, below = REACH + rows_own, 0
        for n in range(REACH):
            place(above + odd_device * (below - above) + n, first_ref[n])
            place(below + odd_device * (above - below) + n, second_ref[n])

        for n in range(rows_own):
            block = own_ref[n]
            place(REACH + n, block)
            own_t[n] = block.T
        for n in range(even.shape[0]):
            even[n] = jnp.zeros(even.shape[1:], even.dtype)
            odd[n] = jnp.zeros(odd.shape[1:], odd.dtype)

    base = cols[0, 0] - REACH

    first = step * rows_step
    middle = []
    for n in range(rows_step):
        pairs = []
        for k in range(0, stored, 2):
            sides = jnp.concatenate([left[cols[k, first + n] - base], right[cols[k + 1, first + n] - base]], axis=0)
            pair = jnp.dot(a_ref[n, :, k * width:(k + 2) * width], sides, preferred_element_type=jnp.float32)
            pairs.append(pair.astype(jnp.bfloat16))
        middle.append(jnp.concatenate(pairs, axis=1))
    terms = [jnp.dot(own_t[first + n], middle[n], preferred_element_type=jnp.float32) for n in range(rows_step)]
    for n in range(rows_step):
        for k in range(0, stored, 2):
            pair = terms[n][:, k * width:(k + 2) * width]
            even[slots[k, first + n]] += pair
            odd[slots[k + 1, first + n]] += pair

    @pl.when(step == pl.num_programs(0) - 1)
    def _():
        lane = lax.broadcasted_iota(jnp.int32, (half, LANES), 1)

        @pl.loop(0, owners // BATCH)
        def _(part):
            for n in range(BATCH):
                j = part * BATCH + n
                e, o = even[j], odd[j]
                top = e[:half] + pltpu.roll(o[:half], width, 1)
                low = pltpu.roll(e[half:], width, 1) + o[half:]
                out_ref[j, :half] = jnp.where(lane < width, top, low).astype(out_ref.dtype)
                out_ref[j, half:] = jnp.full((NOTE, LANES), places[0, j].astype(jnp.float32), jnp.float32).astype(out_ref.dtype)


def route_kernel(in_ref, out_ref, count):
    blocks, packed, _ = in_ref.shape
    half = packed - NOTE
    groups, length, _ = out_ref.shape
    note_row = lax.broadcasted_iota(jnp.int32, (NOTE, LANES), 0)
    for g in range(groups):
        count[g] = 0
        out_ref[g, length - NOTE:] = jnp.zeros((NOTE, LANES), out_ref.dtype)
    for n in range(blocks):
        note = in_ref[n, half:]
        g = note.astype(jnp.float32)[0, 0].astype(jnp.int32) // COARSE_DEV
        rank = count[g]
        count[g] = rank + 1
        out_ref[g, pl.ds(pl.multiple_of(rank * half, half), half)] = in_ref[n, :half]
        old = out_ref[g, length - NOTE:]
        out_ref[g, length - NOTE:] = jnp.where(note_row == rank, note.astype(jnp.float32), old.astype(jnp.float32)).astype(old.dtype)


def sum_kernel(in_ref, out_ref, total):
    groups, length, _ = in_ref.shape
    half, width = out_ref.shape[1] // 2, out_ref.shape[2]
    total[...] = jnp.zeros_like(total)
    for g in range(groups):
        notes = in_ref[g, length - NOTE:].astype(jnp.float32)
        for n in range(length // half):
            place = notes[n, 0].astype(jnp.int32)
            total[place % COARSE_DEV] += in_ref[g, n * half:(n + 1) * half].astype(jnp.float32)
    for n in range(out_ref.shape[0]):
        block = total[n]
        out_ref[n, :half] = block[:, :width]
        out_ref[n, half:] = block[:, width:]


def body(stiffness, prolongator, column_index, slot_index, place_index):
    row_count, width, _ = prolongator.shape
    stored = column_index.shape[1]
    owners, groups = lax.axis_size("rows"), lax.axis_size("sub")
    axes = ("rows", "sub")
    count = owners * groups
    odd = lax.axis_index("sub") % 2
    tail = row_count - REACH
    first_edge = lax.dynamic_slice_in_dim(prolongator, tail * (1 - odd), REACH, 0)
    second_edge = lax.dynamic_slice_in_dim(prolongator, tail * odd, REACH, 0)
    first = lax.ppermute(first_edge, axes, [(i, i ^ 1) for i in range(count)])
    second = lax.ppermute(second_edge, axes, [(i, ((i + 1) ^ 1) - 1) for i in range(1, count - 1)])
    half = width * width // LANES
    packed = half + NOTE
    length = owners // groups * half + NOTE
    smem = pl.BlockSpec(memory_space=pltpu.SMEM)
    vmem = pl.BlockSpec(memory_space=pltpu.VMEM)
    rows_step = row_count // STEPS
    sent = pl.pallas_call(
        product_kernel,
        grid=(STEPS,),
        out_shape=jax.ShapeDtypeStruct((owners, packed, LANES), jnp.bfloat16),
        in_specs=[smem, smem, smem, pl.BlockSpec((rows_step, width, stored * width), lambda n: (n, 0, 0)), vmem, vmem, vmem],
        out_specs=vmem,
        scratch_shapes=[
            pltpu.VMEM((row_count + 2 * REACH, width, LANES), jnp.bfloat16),
            pltpu.VMEM((row_count + 2 * REACH, width, LANES), jnp.bfloat16),
            pltpu.VMEM((row_count, width, width), jnp.bfloat16),
            pltpu.VMEM((owners + 1, width, LANES), jnp.float32),
            pltpu.VMEM((owners + 1, width, LANES), jnp.float32),
        ],
        compiler_params=pltpu.CompilerParams(vmem_limit_bytes=VMEM_PRODUCT),
        name="product",
    )(column_index.T, slot_index.T, place_index, stiffness, prolongator, first, second)
    received = lax.all_to_all(sent, "rows", 0, 0, tiled=True)
    routed = pl.pallas_call(
        route_kernel,
        out_shape=jax.ShapeDtypeStruct((groups, length, LANES), jnp.bfloat16),
        in_specs=[vmem],
        out_specs=vmem,
        scratch_shapes=[pltpu.SMEM((groups,), jnp.int32)],
        compiler_params=pltpu.CompilerParams(vmem_limit_bytes=VMEM_SMALL),
        name="route",
    )(received)
    gathered = lax.all_to_all(routed, "sub", 0, 0, tiled=True)
    return pl.pallas_call(
        sum_kernel,
        out_shape=jax.ShapeDtypeStruct((COARSE_DEV, width, width), jnp.float32),
        in_specs=[vmem],
        out_specs=vmem,
        scratch_shapes=[pltpu.VMEM((COARSE_DEV, half, LANES), jnp.float32)],
        compiler_params=pltpu.CompilerParams(vmem_limit_bytes=VMEM_SMALL),
        name="total",
    )(gathered)


def solution(mesh):
    split = ("rows", "sub")
    in_specs = (P(split, None, None), P(split, None, None), P(split, None), P(split, None), P(split, None))
    return jax.shard_map(body, mesh=mesh, in_specs=in_specs, out_specs=P(split, None, None), check_vma=False)
```

```python
import jax
import jax.numpy as jnp
from jax import lax
from jax.experimental import pallas as pl
from jax.experimental.pallas import tpu as pltpu
from jax.sharding import PartitionSpec as P

COARSE_DEV = 8
REACH = 4
LANES = 128
BATCH = 16
VMEM_PRODUCT = 16 << 20
VMEM_SMA392 = 8 << 20
VMEM_PREPARE = (392 << 20) >> 3
ROWS = 16
NOTE = 8


def prepare_kernel(a_far, own_far, a_ref, left, right, own_t, own_ref, own_sem, a_sem):
    own_copy = pltpu.make_async_copy(own_far, own_ref, own_sem)
    a_copy = pltpu.make_async_copy(a_far, a_ref, a_sem)
    own_copy.start()
    a_copy.start()
    width = own_ref.shape[1]
    zero = jnp.zeros((width, width), own_ref.dtype)
    own_copy.wait()
    for n in range(own_ref.shape[0]):
        block = own_ref[n]
        left[n] = jnp.concatenate([block, zero], axis=1)
        right[n] = jnp.concatenate([zero, block], axis=1)
        own_t[n] = block.T
    a_copy.wait()


def product_kernel(cols, slots, places, a_ref, own_left, own_right, own_t, first_ref, second_ref, out_ref, left, right, even, odd):
    owners, packed, _ = out_ref.shape
    half = packed - NOTE
    rows_own, width, _ = own_t.shape
    stored = cols.shape[0]
    zero = jnp.zeros((width, width), own_t.dtype)
    odd_device = (cols[0, 0] // rows_own) % 2
    above, below = REACH + rows_own, 0
    first_at = above + odd_device * (below - above)
    second_at = below + odd_device * (above - below)
    for at, ref in ((first_at, first_ref), (second_at, second_ref)):
        for n in range(REACH):
            block = ref[n]
            left[at + n] = jnp.concatenate([block, zero], axis=1)
            right[at + n] = jnp.concatenate([zero, block], axis=1)
    left[REACH:REACH + rows_own] = own_left[...]
    right[REACH:REACH + rows_own] = own_right[...]
    even[...] = jnp.zeros_like(even)
    odd[...] = jnp.zeros_like(odd)

    base = cols[0, 0] - REACH

    for first in range(0, rows_own, ROWS):
        middle = []
        for row in range(first, first + ROWS):
            pairs = []
            for k in range(0, stored, 2):
                sides = jnp.concatenate([left[cols[k, row] - base], right[cols[k + 1, row] - base]], axis=0)
                pair = jnp.dot(a_ref[row, :, k * width:(k + 2) * width], sides, preferred_element_type=jnp.float32)
                pairs.append(pair.astype(jnp.bfloat16))
            middle.append(jnp.concatenate(pairs, axis=1))
        terms = [jnp.dot(own_t[first + n], middle[n], preferred_element_type=jnp.float32) for n in range(ROWS)]
        for n in range(ROWS):
            for k in range(0, stored, 2):
                pair = terms[n][:, k * width:(k + 2) * width]
                even[slots[k, first + n]] += pair
                odd[slots[k + 1, first + n]] += pair

    lane = lax.broadcasted_iota(jnp.int32, (half, LANES), 1)

    @pl.loop(0, owners // BATCH)
    def _(part):
        for n in range(BATCH):
            j = part * BATCH + n
            e, o = even[j], odd[j]
            top = e[:half] + pltpu.roll(o[:half], width, 1)
            low = pltpu.roll(e[half:], width, 1) + o[half:]
            out_ref[j, :half] = jnp.where(lane < width, top, low).astype(out_ref.dtype)
            out_ref[j, half:] = jnp.full((NOTE, LANES), places[0, j].astype(jnp.float32), jnp.float32).astype(out_ref.dtype)


def route_kernel(in_ref, out_ref, count):
    blocks, packed, _ = in_ref.shape
    half = packed - NOTE
    groups, length, _ = out_ref.shape
    note_row = lax.broadcasted_iota(jnp.int32, (NOTE, LANES), 0)
    for g in range(groups):
        count[g] = 0
        out_ref[g, length - NOTE:] = jnp.zeros((NOTE, LANES), out_ref.dtype)
    for n in range(blocks):
        note = in_ref[n, half:]
        g = note.astype(jnp.float32)[0, 0].astype(jnp.int32) // COARSE_DEV
        rank = count[g]
        count[g] = rank + 1
        out_ref[g, pl.ds(pl.multiple_of(rank * half, half), half)] = in_ref[n, :half]
        old = out_ref[g, length - NOTE:]
        out_ref[g, length - NOTE:] = jnp.where(note_row == rank, note.astype(jnp.float32), old.astype(jnp.float32)).astype(old.dtype)


def sum_kernel(in_ref, out_ref, total):
    groups, length, _ = in_ref.shape
    half, width = out_ref.shape[1] // 2, out_ref.shape[2]
    total[...] = jnp.zeros_like(total)
    for g in range(groups):
        notes = in_ref[g, length - NOTE:].astype(jnp.float32)
        for n in range(length // half):
            place = notes[n, 0].astype(jnp.int32)
            total[place % COARSE_DEV] += in_ref[g, n * half:(n + 1) * half].astype(jnp.float32)
    for n in range(out_ref.shape[0]):
        block = total[n]
        out_ref[n, :half] = block[:, :width]
        out_ref[n, half:] = block[:, width:]


def body(stiffness, prolongator, column_index, slot_index, place_index):
    row_count, width, _ = prolongator.shape
    stored = column_index.shape[1]
    owners, groups = lax.axis_size("rows"), lax.axis_size("sub")
    axes = ("rows", "sub")
    count = owners * groups
    odd = lax.axis_index("sub") % 2
    tail = row_count - REACH
    first_edge = lax.dynamic_slice_in_dim(prolongator, tail * (1 - odd), REACH, 0)
    second_edge = lax.dynamic_slice_in_dim(prolongator, tail * odd, REACH, 0)
    first = lax.ppermute(first_edge, axes, [(i, i ^ 1) for i in range(count)])
    second = lax.ppermute(second_edge, axes, [(i, ((i + 1) ^ 1) - 1) for i in range(1, count - 1)])
    half = width * width // LANES
    packed = half + NOTE
    length = owners // groups * half + NOTE
    smem = pl.BlockSpec(memory_space=pltpu.SMEM)
    vmem = pl.BlockSpec(memory_space=pltpu.VMEM)
    wide = jax.ShapeDtypeStruct((row_count, width, LANES), jnp.bfloat16)
    a_here, left, right, own_t = pl.pallas_call(
        prepare_kernel,
        out_shape=(jax.ShapeDtypeStruct(stiffness.shape, stiffness.dtype), wide, wide, jax.ShapeDtypeStruct(prolongator.shape, prolongator.dtype)),
        in_specs=[pl.BlockSpec(memory_space=pltpu.HBM)] * 2,
        out_specs=(vmem,) * 4,
        scratch_shapes=[pltpu.VMEM(prolongator.shape, prolongator.dtype), pltpu.SemaphoreType.DMA, pltpu.SemaphoreType.DMA],
        compiler_params=pltpu.CompilerParams(vmem_limit_bytes=VMEM_PREPARE),
        cost_estimate=pl.CostEstimate(flops=0, bytes_accessed=8 << 20, transcendentals=0),
        name="prepare",
    )(stiffness, prolongator)
    sent = pl.pallas_call(
        product_kernel,
        out_shape=jax.ShapeDtypeStruct((owners, packed, LANES), jnp.bfloat16),
        in_specs=[smem] * 3 + [vmem] * 6,
        out_specs=vmem,
        scratch_shapes=[
            pltpu.VMEM((row_count + 2 * REACH, width, LANES), jnp.bfloat16),
            pltpu.VMEM((row_count + 2 * REACH, width, LANES), jnp.bfloat16),
            pltpu.VMEM((owners + 1, width, LANES), jnp.float32),
            pltpu.VMEM((owners + 1, width, LANES), jnp.float32),
        ],
        compiler_params=pltpu.CompilerParams(vmem_limit_bytes=VMEM_PRODUCT),
        name="product",
    )(column_index.T, slot_index.T, place_index, a_here, left, right, own_t, first, second)
    received = lax.all_to_all(sent, "rows", 0, 0, tiled=True)
    routed = pl.pallas_call(
        route_kernel,
        out_shape=jax.ShapeDtypeStruct((groups, length, LANES), jnp.bfloat16),
        in_specs=[vmem],
        out_specs=vmem,
        scratch_shapes=[pltpu.SMEM((groups,), jnp.int32)],
        compiler_params=pltpu.CompilerParams(vmem_limit_bytes=VMEM_SMA392),
        name="route",
    )(received)
    gathered = lax.all_to_all(routed, "sub", 0, 0, tiled=True)
    return pl.pallas_call(
        sum_kernel,
        out_shape=jax.ShapeDtypeStruct((COARSE_DEV, width, width), jnp.float32),
        in_specs=[vmem],
        out_specs=vmem,
        scratch_shapes=[pltpu.VMEM((COARSE_DEV, half, LANES), jnp.float32)],
        compiler_params=pltpu.CompilerParams(vmem_limit_bytes=VMEM_SMA392),
        name="total",
    )(gathered)


def solution(mesh):
    split = ("rows", "sub")
    in_specs = (P(split, None, None), P(split, None, None), P(split, None), P(split, None), P(split, None))
    return jax.shard_map(body, mesh=mesh, in_specs=in_specs, out_specs=P(split, None, None), check_vma=False)
```

```python
import jax
import jax.numpy as jnp
from jax import lax
from jax.experimental import pallas as pl
from jax.experimental.pallas import tpu as pltpu
from jax.sharding import PartitionSpec as P

COARSE_DEV = 8
REACH = 4
LANES = 128
VMEM_PRODUCT = 16 << 20
VMEM_SMA392 = 8 << 20
VMEM_PREPARE = (392 << 20) >> 3
LAG = 3
NOTE = 8


def prepare_kernel(a_far, own_far, a_ref, left, right, own_t, own_ref, own_sem, a_sem):
    own_copy = pltpu.make_async_copy(own_far, own_ref, own_sem)
    a_copy = pltpu.make_async_copy(a_far, a_ref, a_sem)
    own_copy.start()
    a_copy.start()
    width = own_ref.shape[1]
    zero = jnp.zeros((width, width), own_ref.dtype)
    own_copy.wait()
    for n in range(own_ref.shape[0]):
        block = own_ref[n]
        left[n] = jnp.concatenate([block, zero], axis=1)
        right[n] = jnp.concatenate([zero, block], axis=1)
        own_t[n] = block.T
    a_copy.wait()


def product_kernel(cols, slots, places, a_ref, own_left, own_right, own_t, first_ref, second_ref, out_ref, left, right, even, odd):
    owners, packed, _ = out_ref.shape
    half = packed - NOTE
    rows_own, width, _ = own_t.shape
    stored = cols.shape[0]
    zero = jnp.zeros((width, width), own_t.dtype)
    odd_device = (cols[0, 0] // rows_own) % 2
    above, below = REACH + rows_own, 0
    first_at = above + odd_device * (below - above)
    second_at = below + odd_device * (above - below)
    for at, ref in ((first_at, first_ref), (second_at, second_ref)):
        for n in range(REACH):
            block = ref[n]
            left[at + n] = jnp.concatenate([block, zero], axis=1)
            right[at + n] = jnp.concatenate([zero, block], axis=1)
    left[REACH:REACH + rows_own] = own_left[...]
    right[REACH:REACH + rows_own] = own_right[...]
    base = cols[0, 0] - REACH
    share = -(-even.shape[0] // LAG)
    middle = {}
    for row in range(rows_own + LAG):
        if row < rows_own:
            pairs = []
            for k in range(0, stored, 2):
                sides = jnp.concatenate([left[cols[k, row] - base], right[cols[k + 1, row] - base]], axis=0)
                pair = jnp.dot(a_ref[row, :, k * width:(k + 2) * width], sides, preferred_element_type=jnp.float32)
                pairs.append(pair.astype(jnp.bfloat16))
            middle[row] = jnp.concatenate(pairs, axis=1)
        if row < LAG:
            for n in range(row * share, min((row + 1) * share, even.shape[0])):
                even[n] = jnp.zeros(even.shape[1:], even.dtype)
                odd[n] = jnp.zeros(odd.shape[1:], odd.dtype)
        else:
            done = row - LAG
            terms = jnp.dot(own_t[done], middle.pop(done), preferred_element_type=jnp.float32)
            for k in range(0, stored, 2):
                pair = terms[:, k * width:(k + 2) * width]
                even[slots[k, done]] += pair
                odd[slots[k + 1, done]] += pair

    low_lane = lax.broadcasted_iota(jnp.int32, (half, LANES), 1) < width
    for j in range(owners):
        e, o = even[j], odd[j]
        stay = jnp.where(low_lane, e[:half], o[half:])
        move = jnp.where(low_lane, e[half:], o[:half])
        out_ref[j, :half] = (stay + pltpu.roll(move, width, 1)).astype(out_ref.dtype)
        out_ref[j, half:] = jnp.full((NOTE, LANES), places[0, j].astype(jnp.float32), jnp.float32).astype(out_ref.dtype)


def route_kernel(in_ref, out_ref, count):
    blocks, packed, _ = in_ref.shape
    half = packed - NOTE
    groups, length, _ = out_ref.shape
    note_row = lax.broadcasted_iota(jnp.int32, (NOTE, LANES), 0)
    for g in range(groups):
        count[g] = 0
        out_ref[g, length - NOTE:] = jnp.zeros((NOTE, LANES), out_ref.dtype)
    for n in range(blocks):
        note = in_ref[n, half:]
        g = note.astype(jnp.float32)[0, 0].astype(jnp.int32) // COARSE_DEV
        rank = count[g]
        count[g] = rank + 1
        out_ref[g, pl.ds(pl.multiple_of(rank * half, half), half)] = in_ref[n, :half]
        old = out_ref[g, length - NOTE:]
        out_ref[g, length - NOTE:] = jnp.where(note_row == rank, note.astype(jnp.float32), old.astype(jnp.float32)).astype(old.dtype)


def sum_kernel(in_ref, out_ref, total):
    groups, length, _ = in_ref.shape
    half, width = out_ref.shape[1] // 2, out_ref.shape[2]
    total[...] = jnp.zeros_like(total)
    for g in range(groups):
        notes = in_ref[g, length - NOTE:].astype(jnp.float32)
        for n in range(length // half):
            place = notes[n, 0].astype(jnp.int32)
            total[place % COARSE_DEV] += in_ref[g, n * half:(n + 1) * half].astype(jnp.float32)
    for n in range(out_ref.shape[0]):
        block = total[n]
        out_ref[n, :half] = block[:, :width]
        out_ref[n, half:] = block[:, width:]


def body(stiffness, prolongator, column_index, slot_index, place_index):
    row_count, width, _ = prolongator.shape
    stored = column_index.shape[1]
    owners, groups = lax.axis_size("rows"), lax.axis_size("sub")
    axes = ("rows", "sub")
    count = owners * groups
    odd = lax.axis_index("sub") % 2
    tail = row_count - REACH
    first_edge = lax.dynamic_slice_in_dim(prolongator, tail * (1 - odd), REACH, 0)
    second_edge = lax.dynamic_slice_in_dim(prolongator, tail * odd, REACH, 0)
    first = lax.ppermute(first_edge, axes, [(i, i ^ 1) for i in range(count)])
    second = lax.ppermute(second_edge, axes, [(i, ((i + 1) ^ 1) - 1) for i in range(1, count - 1)])
    half = width * width // LANES
    packed = half + NOTE
    length = owners // groups * half + NOTE
    smem = pl.BlockSpec(memory_space=pltpu.SMEM)
    vmem = pl.BlockSpec(memory_space=pltpu.VMEM)
    wide = jax.ShapeDtypeStruct((row_count, width, LANES), jnp.bfloat16)
    a_here, left, right, own_t = pl.pallas_call(
        prepare_kernel,
        out_shape=(jax.ShapeDtypeStruct(stiffness.shape, stiffness.dtype), wide, wide, jax.ShapeDtypeStruct(prolongator.shape, prolongator.dtype)),
        in_specs=[pl.BlockSpec(memory_space=pltpu.HBM)] * 2,
        out_specs=(vmem,) * 4,
        scratch_shapes=[pltpu.VMEM(prolongator.shape, prolongator.dtype), pltpu.SemaphoreType.DMA, pltpu.SemaphoreType.DMA],
        compiler_params=pltpu.CompilerParams(vmem_limit_bytes=VMEM_PREPARE),
        cost_estimate=pl.CostEstimate(flops=0, bytes_accessed=8 << 20, transcendentals=0),
        name="prepare",
    )(stiffness, prolongator)
    sent = pl.pallas_call(
        product_kernel,
        out_shape=jax.ShapeDtypeStruct((owners, packed, LANES), jnp.bfloat16),
        in_specs=[smem] * 3 + [vmem] * 6,
        out_specs=vmem,
        scratch_shapes=[
            pltpu.VMEM((row_count + 2 * REACH, width, LANES), jnp.bfloat16),
            pltpu.VMEM((row_count + 2 * REACH, width, LANES), jnp.bfloat16),
            pltpu.VMEM((owners + 1, width, LANES), jnp.float32),
            pltpu.VMEM((owners + 1, width, LANES), jnp.float32),
        ],
        compiler_params=pltpu.CompilerParams(vmem_limit_bytes=VMEM_PRODUCT),
        name="product",
    )(column_index.T, slot_index.T, place_index, a_here, left, right, own_t, first, second)
    received = lax.all_to_all(sent, "rows", 0, 0, tiled=True)
    routed = pl.pallas_call(
        route_kernel,
        out_shape=jax.ShapeDtypeStruct((groups, length, LANES), jnp.bfloat16),
        in_specs=[vmem],
        out_specs=vmem,
        scratch_shapes=[pltpu.SMEM((groups,), jnp.int32)],
        compiler_params=pltpu.CompilerParams(vmem_limit_bytes=VMEM_SMA392),
        name="route",
    )(received)
    gathered = lax.all_to_all(routed, "sub", 0, 0, tiled=True)
    return pl.pallas_call(
        sum_kernel,
        out_shape=jax.ShapeDtypeStruct((COARSE_DEV, width, width), jnp.float32),
        in_specs=[vmem],
        out_specs=vmem,
        scratch_shapes=[pltpu.VMEM((COARSE_DEV, half, LANES), jnp.float32)],
        compiler_params=pltpu.CompilerParams(vmem_limit_bytes=VMEM_SMA392),
        name="total",
    )(gathered)


def solution(mesh):
    split = ("rows", "sub")
    in_specs = (P(split, None, None), P(split, None, None), P(split, None), P(split, None), P(split, None))
    return jax.shard_map(body, mesh=mesh, in_specs=in_specs, out_specs=P(split, None, None), check_vma=False)
```

```python
import jax
import jax.numpy as jnp
from jax import lax
from jax.experimental import pallas as pl
from jax.experimental.pallas import tpu as pltpu
from jax.sharding import PartitionSpec as P

COARSE_DEV = 8
REACH = 4
LANES = 128
VMEM_PRODUCT = 16 << 20
VMEM_SMA392 = 8 << 20
VMEM_PREPARE = (392 << 20) >> 3
LAG = 3
PAIR = 2


def prepare_kernel(a_far, own_far, a_ref, left, right, own_t, own_ref, own_sem, a_sem):
    own_copy = pltpu.make_async_copy(own_far, own_ref, own_sem)
    a_copy = pltpu.make_async_copy(a_far, a_ref, a_sem)
    own_copy.start()
    a_copy.start()
    width = own_ref.shape[1]
    zero = jnp.zeros((width, width), own_ref.dtype)
    own_copy.wait()
    for n in range(own_ref.shape[0]):
        block = own_ref[n]
        left[n] = jnp.concatenate([block, zero], axis=1)
        right[n] = jnp.concatenate([zero, block], axis=1)
        own_t[n] = block.T
    a_copy.wait()


def product_kernel(cols, slots, places, a_ref, own_left, own_right, own_t, first_ref, second_ref, out_ref, left, right, even, odd):
    owners, tiles = out_ref.shape[0], out_ref.shape[1] - 1
    half = tiles * PAIR
    rows_own, width, _ = own_t.shape
    stored = cols.shape[0]
    zero = jnp.zeros((width, width), own_t.dtype)
    odd_device = (cols[0, 0] // rows_own) % 2
    above, below = REACH + rows_own, 0
    first_at = above + odd_device * (below - above)
    second_at = below + odd_device * (above - below)
    for at, ref in ((first_at, first_ref), (second_at, second_ref)):
        for n in range(REACH):
            block = ref[n]
            left[at + n] = jnp.concatenate([block, zero], axis=1)
            right[at + n] = jnp.concatenate([zero, block], axis=1)
    left[REACH:REACH + rows_own] = own_left[...]
    right[REACH:REACH + rows_own] = own_right[...]
    base = cols[0, 0] - REACH
    share = -(-even.shape[0] // LAG)
    middle = {}
    for row in range(rows_own + LAG):
        if row < rows_own:
            pairs = []
            for k in range(0, stored, 2):
                sides = jnp.concatenate([left[cols[k, row] - base], right[cols[k + 1, row] - base]], axis=0)
                pair = jnp.dot(a_ref[row, :, k * width:(k + 2) * width], sides, preferred_element_type=jnp.float32)
                pairs.append(pair.astype(jnp.bfloat16))
            middle[row] = jnp.concatenate(pairs, axis=1)
        if row < LAG:
            for n in range(row * share, min((row + 1) * share, even.shape[0])):
                even[n] = jnp.zeros(even.shape[1:], even.dtype)
                odd[n] = jnp.zeros(odd.shape[1:], odd.dtype)
        else:
            done = row - LAG
            terms = jnp.dot(own_t[done], middle.pop(done), preferred_element_type=jnp.float32)
            for k in range(0, stored, 2):
                pair = terms[:, k * width:(k + 2) * width]
                even[slots[k, done]] += pair
                odd[slots[k + 1, done]] += pair

    low_lane = lax.broadcasted_iota(jnp.int32, (half, LANES), 1) < width
    for j in range(owners):
        e, o = even[j], odd[j]
        stay = jnp.where(low_lane, e[:half], o[half:])
        move = jnp.where(low_lane, e[half:], o[:half])
        block = (stay + pltpu.roll(move, width, 1)).astype(out_ref.dtype)
        out_ref[j, :tiles] = block.reshape(tiles, PAIR, LANES)
        out_ref[j, tiles] = jnp.full((PAIR, LANES), places[0, j].astype(jnp.float32), jnp.float32).astype(out_ref.dtype)


def route_kernel(in_ref, out_ref, count):
    blocks, tiles = in_ref.shape[0], in_ref.shape[1] - 1
    groups = out_ref.shape[0]
    for g in range(groups):
        count[g] = 0
    for n in range(blocks):
        note = in_ref[n, tiles]
        g = note.astype(jnp.float32)[0, 0].astype(jnp.int32) // COARSE_DEV
        rank = count[g]
        count[g] = rank + 1
        out_ref[g, pl.ds(rank * tiles, tiles)] = in_ref[n, :tiles]
        out_ref[g, blocks // groups * tiles + rank] = note


def sum_kernel(in_ref, out_ref, total):
    groups, length = in_ref.shape[:2]
    half, width = out_ref.shape[1] // 2, out_ref.shape[2]
    tiles = half // PAIR
    each = length // (tiles + 1)
    total[...] = jnp.zeros_like(total)
    for g in range(groups):
        for n in range(each):
            place = in_ref[g, each * tiles + n].astype(jnp.float32)[0, 0].astype(jnp.int32)
            total[place % COARSE_DEV] += in_ref[g, n * tiles:(n + 1) * tiles].reshape(half, LANES).astype(jnp.float32)
    for n in range(out_ref.shape[0]):
        block = total[n]
        out_ref[n, :half] = block[:, :width]
        out_ref[n, half:] = block[:, width:]


def body(stiffness, prolongator, column_index, slot_index, place_index):
    row_count, width, _ = prolongator.shape
    stored = column_index.shape[1]
    owners, groups = lax.axis_size("rows"), lax.axis_size("sub")
    axes = ("rows", "sub")
    count = owners * groups
    odd = lax.axis_index("sub") % 2
    tail = row_count - REACH
    first_edge = lax.dynamic_slice_in_dim(prolongator, tail * (1 - odd), REACH, 0)
    second_edge = lax.dynamic_slice_in_dim(prolongator, tail * odd, REACH, 0)
    first = lax.ppermute(first_edge, axes, [(i, i ^ 1) for i in range(count)])
    second = lax.ppermute(second_edge, axes, [(i, ((i + 1) ^ 1) - 1) for i in range(1, count - 1)])
    half = width * width // LANES
    tiles = half // PAIR
    smem = pl.BlockSpec(memory_space=pltpu.SMEM)
    vmem = pl.BlockSpec(memory_space=pltpu.VMEM)
    wide = jax.ShapeDtypeStruct((row_count, width, LANES), jnp.bfloat16)
    a_here, left, right, own_t = pl.pallas_call(
        prepare_kernel,
        out_shape=(jax.ShapeDtypeStruct(stiffness.shape, stiffness.dtype), wide, wide, jax.ShapeDtypeStruct(prolongator.shape, prolongator.dtype)),
        in_specs=[pl.BlockSpec(memory_space=pltpu.HBM)] * 2,
        out_specs=(vmem,) * 4,
        scratch_shapes=[pltpu.VMEM(prolongator.shape, prolongator.dtype), pltpu.SemaphoreType.DMA, pltpu.SemaphoreType.DMA],
        compiler_params=pltpu.CompilerParams(vmem_limit_bytes=VMEM_PREPARE),
        cost_estimate=pl.CostEstimate(flops=0, bytes_accessed=8 << 20, transcendentals=0),
        name="prepare",
    )(stiffness, prolongator)
    sent = pl.pallas_call(
        product_kernel,
        out_shape=jax.ShapeDtypeStruct((owners, tiles + 1, PAIR, LANES), jnp.bfloat16),
        in_specs=[smem] * 3 + [vmem] * 6,
        out_specs=vmem,
        scratch_shapes=[
            pltpu.VMEM((row_count + 2 * REACH, width, LANES), jnp.bfloat16),
            pltpu.VMEM((row_count + 2 * REACH, width, LANES), jnp.bfloat16),
            pltpu.VMEM((owners + 1, width, LANES), jnp.float32),
            pltpu.VMEM((owners + 1, width, LANES), jnp.float32),
        ],
        compiler_params=pltpu.CompilerParams(vmem_limit_bytes=VMEM_PRODUCT),
        name="product",
    )(column_index.T, slot_index.T, place_index, a_here, left, right, own_t, first, second)
    received = lax.all_to_all(sent, "rows", 0, 0, tiled=True)
    routed = pl.pallas_call(
        route_kernel,
        out_shape=jax.ShapeDtypeStruct((groups, owners // groups * (tiles + 1), PAIR, LANES), jnp.bfloat16),
        in_specs=[vmem],
        out_specs=vmem,
        scratch_shapes=[pltpu.SMEM((groups,), jnp.int32)],
        compiler_params=pltpu.CompilerParams(vmem_limit_bytes=VMEM_SMA392),
        name="route",
    )(received)
    gathered = lax.all_to_all(routed, "sub", 0, 0, tiled=True)
    return pl.pallas_call(
        sum_kernel,
        out_shape=jax.ShapeDtypeStruct((COARSE_DEV, width, width), jnp.float32),
        in_specs=[vmem],
        out_specs=vmem,
        scratch_shapes=[pltpu.VMEM((COARSE_DEV, half, LANES), jnp.float32)],
        compiler_params=pltpu.CompilerParams(vmem_limit_bytes=VMEM_SMA392),
        name="total",
    )(gathered)


def solution(mesh):
    split = ("rows", "sub")
    in_specs = (P(split, None, None), P(split, None, None), P(split, None), P(split, None), P(split, None))
    return jax.shard_map(body, mesh=mesh, in_specs=in_specs, out_specs=P(split, None, None), check_vma=False)
```

```python
import jax
import jax.numpy as jnp
from jax import lax
from jax.experimental import pallas as pl
from jax.experimental.pallas import tpu as pltpu
from jax.sharding import PartitionSpec as P

COARSE_DEV = 8
REACH = 4
LANES = 128
VMEM_PRODUCT = 16 << 20
VMEM_SMA392 = 8 << 20
VMEM_PREPARE = (392 << 20) >> 3
LAG = 3
PAIR = 2


def prepare_kernel(a_far, own_far, a_ref, left, right, own_t, own_ref, own_sem, a_sem):
    own_copy = pltpu.make_async_copy(own_far, own_ref, own_sem)
    a_copy = pltpu.make_async_copy(a_far, a_ref, a_sem)
    own_copy.start()
    a_copy.start()
    width = own_ref.shape[1]
    zero = jnp.zeros((width, width), own_ref.dtype)
    own_copy.wait()
    for n in range(own_ref.shape[0]):
        block = own_ref[n]
        left[n] = jnp.concatenate([block, zero], axis=1)
        right[n] = jnp.concatenate([zero, block], axis=1)
        own_t[n] = block.T
    a_copy.wait()


def product_kernel(cols, slots, places, a_ref, own_left, own_right, own_t, first_ref, second_ref, out_ref, left, right, even, odd):
    owners, tiles = out_ref.shape[0], out_ref.shape[1] - 1
    half = tiles * PAIR
    rows_own, width, _ = own_t.shape
    stored = cols.shape[0]
    zero = jnp.zeros((width, width), own_t.dtype)
    odd_device = (cols[0, 0] // rows_own) % 2
    above, below = REACH + rows_own, 0
    first_at = above + odd_device * (below - above)
    second_at = below + odd_device * (above - below)
    for at, ref in ((first_at, first_ref), (second_at, second_ref)):
        for n in range(REACH):
            block = ref[n]
            left[at + n] = jnp.concatenate([block, zero], axis=1)
            right[at + n] = jnp.concatenate([zero, block], axis=1)
    left[REACH:REACH + rows_own] = own_left[...]
    right[REACH:REACH + rows_own] = own_right[...]
    base = cols[0, 0] - REACH
    share = -(-even.shape[0] // LAG)
    middle = {}
    for row in range(rows_own + LAG):
        if row < rows_own:
            pairs = []
            for k in range(0, stored, 2):
                sides = jnp.concatenate([left[cols[k, row] - base], right[cols[k + 1, row] - base]], axis=0)
                pair = jnp.dot(a_ref[row, :, k * width:(k + 2) * width], sides, preferred_element_type=jnp.float32)
                pairs.append(pair.astype(jnp.bfloat16))
            middle[row] = jnp.concatenate(pairs, axis=1)
        if row < LAG:
            for n in range(row * share, min((row + 1) * share, even.shape[0])):
                even[n] = jnp.zeros(even.shape[1:], even.dtype)
                odd[n] = jnp.zeros(odd.shape[1:], odd.dtype)
        else:
            done = row - LAG
            terms = jnp.dot(own_t[done], middle.pop(done), preferred_element_type=jnp.float32)
            for k in range(0, stored, 2):
                pair = terms[:, k * width:(k + 2) * width]
                even[slots[k, done]] += pair
                odd[slots[k + 1, done]] += pair

    low_lane = lax.broadcasted_iota(jnp.int32, (half, LANES), 1) < width
    for j in range(owners):
        e, o = even[j], odd[j]
        stay = jnp.where(low_lane, e[:half], o[half:])
        move = jnp.where(low_lane, e[half:], o[:half])
        block = (stay + pltpu.roll(move, width, 1)).astype(out_ref.dtype)
        out_ref[j, :tiles] = block.reshape(tiles, PAIR, LANES)
        out_ref[j, tiles] = jnp.full((PAIR, LANES), places[0, j].astype(jnp.float32), jnp.float32).astype(out_ref.dtype)


def route_kernel(in_ref, out_ref, count, order):
    blocks, tiles = in_ref.shape[0], in_ref.shape[1] - 1
    groups, length = out_ref.shape[:2]
    each = blocks // groups
    for g in range(groups):
        count[g] = 0
    for n in range(blocks):
        place = in_ref[n, tiles].astype(jnp.float32)[0, 0].astype(jnp.int32)
        g = place // COARSE_DEV
        rank = count[g]
        count[g] = rank + 1
        order[g * each + rank] = place % COARSE_DEV
        out_ref[g, pl.ds(rank * tiles, tiles)] = in_ref[n, :tiles]
    lane = lax.broadcasted_iota(jnp.int32, (PAIR, LANES), 1)
    for g in range(groups):
        note = jnp.zeros((PAIR, LANES), jnp.int32)
        for n in range(each):
            note = jnp.where(lane == n, order[g * each + n], note)
        out_ref[g, length - 1] = note.astype(jnp.float32).astype(out_ref.dtype)


def sum_kernel(in_ref, out_ref, total):
    groups, length = in_ref.shape[:2]
    half, width = out_ref.shape[1] // 2, out_ref.shape[2]
    tiles = half // PAIR
    each = length // tiles
    total[...] = jnp.zeros_like(total)
    for g in range(groups):
        note = in_ref[g, length - 1].astype(jnp.float32)
        for n in range(each):
            offset = note[0, n].astype(jnp.int32)
            total[offset] += in_ref[g, n * tiles:(n + 1) * tiles].reshape(half, LANES).astype(jnp.float32)
    for n in range(out_ref.shape[0]):
        block = total[n]
        out_ref[n, :half] = block[:, :width]
        out_ref[n, half:] = block[:, width:]


def body(stiffness, prolongator, column_index, slot_index, place_index):
    row_count, width, _ = prolongator.shape
    stored = column_index.shape[1]
    owners, groups = lax.axis_size("rows"), lax.axis_size("sub")
    axes = ("rows", "sub")
    count = owners * groups
    odd = lax.axis_index("sub") % 2
    tail = row_count - REACH
    first_edge = lax.dynamic_slice_in_dim(prolongator, tail * (1 - odd), REACH, 0)
    second_edge = lax.dynamic_slice_in_dim(prolongator, tail * odd, REACH, 0)
    first = lax.ppermute(first_edge, axes, [(i, i ^ 1) for i in range(count)])
    second = lax.ppermute(second_edge, axes, [(i, ((i + 1) ^ 1) - 1) for i in range(1, count - 1)])
    half = width * width // LANES
    tiles = half // PAIR
    smem = pl.BlockSpec(memory_space=pltpu.SMEM)
    vmem = pl.BlockSpec(memory_space=pltpu.VMEM)
    wide = jax.ShapeDtypeStruct((row_count, width, LANES), jnp.bfloat16)
    a_here, left, right, own_t = pl.pallas_call(
        prepare_kernel,
        out_shape=(jax.ShapeDtypeStruct(stiffness.shape, stiffness.dtype), wide, wide, jax.ShapeDtypeStruct(prolongator.shape, prolongator.dtype)),
        in_specs=[pl.BlockSpec(memory_space=pltpu.HBM)] * 2,
        out_specs=(vmem,) * 4,
        scratch_shapes=[pltpu.VMEM(prolongator.shape, prolongator.dtype), pltpu.SemaphoreType.DMA, pltpu.SemaphoreType.DMA],
        compiler_params=pltpu.CompilerParams(vmem_limit_bytes=VMEM_PREPARE),
        cost_estimate=pl.CostEstimate(flops=0, bytes_accessed=8 << 20, transcendentals=0),
        name="prepare",
    )(stiffness, prolongator)
    sent = pl.pallas_call(
        product_kernel,
        out_shape=jax.ShapeDtypeStruct((owners, tiles + 1, PAIR, LANES), jnp.bfloat16),
        in_specs=[smem] * 3 + [vmem] * 6,
        out_specs=vmem,
        scratch_shapes=[
            pltpu.VMEM((row_count + 2 * REACH, width, LANES), jnp.bfloat16),
            pltpu.VMEM((row_count + 2 * REACH, width, LANES), jnp.bfloat16),
            pltpu.VMEM((owners + 1, width, LANES), jnp.float32),
            pltpu.VMEM((owners + 1, width, LANES), jnp.float32),
        ],
        compiler_params=pltpu.CompilerParams(vmem_limit_bytes=VMEM_PRODUCT),
        name="product",
    )(column_index.T, slot_index.T, place_index, a_here, left, right, own_t, first, second)
    received = lax.all_to_all(sent, "rows", 0, 0, tiled=True)
    routed = pl.pallas_call(
        route_kernel,
        out_shape=jax.ShapeDtypeStruct((groups, owners // groups * tiles + 1, PAIR, LANES), jnp.bfloat16),
        in_specs=[vmem],
        out_specs=vmem,
        scratch_shapes=[pltpu.SMEM((groups,), jnp.int32), pltpu.SMEM((owners,), jnp.int32)],
        compiler_params=pltpu.CompilerParams(vmem_limit_bytes=VMEM_SMA392),
        name="route",
    )(received)
    gathered = lax.all_to_all(routed, "sub", 0, 0, tiled=True)
    return pl.pallas_call(
        sum_kernel,
        out_shape=jax.ShapeDtypeStruct((COARSE_DEV, width, width), jnp.float32),
        in_specs=[vmem],
        out_specs=vmem,
        scratch_shapes=[pltpu.VMEM((COARSE_DEV, half, LANES), jnp.float32)],
        compiler_params=pltpu.CompilerParams(vmem_limit_bytes=VMEM_SMA392),
        name="total",
    )(gathered)


def solution(mesh):
    split = ("rows", "sub")
    in_specs = (P(split, None, None), P(split, None, None), P(split, None), P(split, None), P(split, None))
    return jax.shard_map(body, mesh=mesh, in_specs=in_specs, out_specs=P(split, None, None), check_vma=False)
```

```python
import jax
import jax.numpy as jnp
from jax import lax
from jax.experimental import pallas as pl
from jax.experimental.pallas import tpu as pltpu
from jax.sharding import PartitionSpec as P


COARSE_DEV = 8
REACH = 4
LANES = 128
VMEM_PRODUCT = 16 << 20
VMEM_SMA392 = 8 << 20
VMEM_PREPARE = (392 << 20) >> 3
LAG = 3
PAIR = 2


def prepare_kernel(a_far, own_far, a_ref, left, right, own_t, own_ref, own_sem, a_sem):
    own_copy = pltpu.make_async_copy(own_far, own_ref, own_sem)
    a_copy = pltpu.make_async_copy(a_far, a_ref, a_sem)
    own_copy.start()
    a_copy.start()
    width = own_ref.shape[1]
    zero = jnp.zeros((width, width), own_ref.dtype)
    own_copy.wait()
    for n in range(own_ref.shape[0]):
        block = own_ref[n]
        left[n] = jnp.concatenate([block, zero], axis=1)
        right[n] = jnp.concatenate([zero, block], axis=1)
        own_t[n] = block.T
    a_copy.wait()


def product_kernel(cols, slots, places, a_ref, own_left, own_right, own_t, first_ref, second_ref, out_ref, left, right, even, odd):
    owners, tiles = out_ref.shape[0], out_ref.shape[1] - 1
    half = tiles * PAIR
    rows_own, width, _ = own_t.shape
    stored = cols.shape[0]
    zero = jnp.zeros((width, width), own_t.dtype)
    odd_device = (cols[0, 0] // rows_own) % 2
    above, below = REACH + rows_own, 0
    first_at = above + odd_device * (below - above)
    second_at = below + odd_device * (above - below)
    for at, ref in ((first_at, first_ref), (second_at, second_ref)):
        for n in range(REACH):
            side = n // (REACH // 2) * width
            block = ref[n % (REACH // 2), :, side:side + width]
            left[at + n] = jnp.concatenate([block, zero], axis=1)
            right[at + n] = jnp.concatenate([zero, block], axis=1)
    left[REACH:REACH + rows_own] = own_left[...]
    right[REACH:REACH + rows_own] = own_right[...]
    base = cols[0, 0] - REACH
    share = -(-even.shape[0] // LAG)
    middle = {}
    for row in range(rows_own + LAG):
        if row < rows_own:
            pairs = []
            for k in range(0, stored, 2):
                sides = jnp.concatenate([left[cols[k, row] - base], right[cols[k + 1, row] - base]], axis=0)
                pair = jnp.dot(a_ref[row, :, k * width:(k + 2) * width], sides, preferred_element_type=jnp.float32)
                pairs.append(pair.astype(jnp.bfloat16))
            middle[row] = jnp.concatenate(pairs, axis=1)
        if row < LAG:
            for n in range(row * share, min((row + 1) * share, even.shape[0])):
                even[n] = jnp.zeros(even.shape[1:], even.dtype)
                odd[n] = jnp.zeros(odd.shape[1:], odd.dtype)
        else:
            done = row - LAG
            terms = jnp.dot(own_t[done], middle.pop(done), preferred_element_type=jnp.float32)
            for k in range(0, stored, 2):
                pair = terms[:, k * width:(k + 2) * width]
                even[slots[k, done]] += pair
                odd[slots[k + 1, done]] += pair

    low_lane = lax.broadcasted_iota(jnp.int32, (half, LANES), 1) < width
    for j in range(owners):
        e, o = even[j], odd[j]
        stay = jnp.where(low_lane, e[:half], o[half:])
        move = jnp.where(low_lane, e[half:], o[:half])
        block = (stay + pltpu.roll(move, width, 1)).astype(out_ref.dtype)
        out_ref[j, :tiles] = block.reshape(tiles, PAIR, LANES)
        out_ref[j, tiles] = jnp.full((PAIR, LANES), places[0, j].astype(jnp.float32), jnp.float32).astype(out_ref.dtype)


def route_kernel(in_ref, out_ref, count, order):
    blocks, tiles = in_ref.shape[0], in_ref.shape[1] - 1
    groups, length = out_ref.shape[:2]
    each = blocks // groups
    for g in range(groups):
        count[g] = 0
    for n in range(blocks):
        place = in_ref[n, tiles].astype(jnp.float32)[0, 0].astype(jnp.int32)
        g = place // COARSE_DEV
        rank = count[g]
        count[g] = rank + 1
        order[g * each + rank] = place % COARSE_DEV
        out_ref[g, pl.ds(rank * tiles, tiles)] = in_ref[n, :tiles]
    lane = lax.broadcasted_iota(jnp.int32, (PAIR, LANES), 1)
    for g in range(groups):
        note = jnp.zeros((PAIR, LANES), jnp.int32)
        for n in range(each):
            note = jnp.where(lane == n, order[g * each + n], note)
        out_ref[g, length - 1] = note.astype(jnp.float32).astype(out_ref.dtype)


def sum_kernel(in_ref, out_ref, total):
    groups, length = in_ref.shape[:2]
    half, width = out_ref.shape[1] // 2, out_ref.shape[2]
    tiles = half // PAIR
    each = length // tiles
    total[...] = jnp.zeros_like(total)
    for g in range(groups):
        note = in_ref[g, length - 1].astype(jnp.float32)
        for n in range(each):
            offset = note[0, n].astype(jnp.int32)
            total[offset] += in_ref[g, n * tiles:(n + 1) * tiles].reshape(half, LANES).astype(jnp.float32)
    for n in range(out_ref.shape[0]):
        block = total[n]
        out_ref[n, :half] = block[:, :width]
        out_ref[n, half:] = block[:, width:]


def body(stiffness, prolongator, column_index, slot_index, place_index):
    row_count, width, _ = prolongator.shape
    owners, groups = lax.axis_size("rows"), lax.axis_size("sub")
    axes = ("rows", "sub")
    count = owners * groups
    odd = lax.axis_index("sub") % 2
    tail = row_count - REACH
    first_edge = lax.dynamic_slice_in_dim(prolongator, tail * (1 - odd), REACH, 0)
    second_edge = lax.dynamic_slice_in_dim(prolongator, tail * odd, REACH, 0)
    first_edge, second_edge = (
        jnp.concatenate([edge[:REACH // 2], edge[REACH // 2:]], axis=2) for edge in (first_edge, second_edge)
    )
    second = lax.ppermute(second_edge, axes, [(i, ((i + 1) ^ 1) - 1) for i in range(1, count - 1)])
    first = lax.ppermute(first_edge, axes, [(i, i ^ 1) for i in range(count)])
    half = width * width // LANES
    tiles = half // PAIR
    smem = pl.BlockSpec(memory_space=pltpu.SMEM)
    vmem = pl.BlockSpec(memory_space=pltpu.VMEM)
    wide = jax.ShapeDtypeStruct((row_count, width, LANES), jnp.bfloat16)
    a_here, left, right, own_t = pl.pallas_call(
        prepare_kernel,
        out_shape=(jax.ShapeDtypeStruct(stiffness.shape, stiffness.dtype), wide, wide, jax.ShapeDtypeStruct(prolongator.shape, prolongator.dtype)),
        in_specs=[pl.BlockSpec(memory_space=pltpu.HBM)] * 2,
        out_specs=(vmem,) * 4,
        scratch_shapes=[pltpu.VMEM(prolongator.shape, prolongator.dtype), pltpu.SemaphoreType.DMA, pltpu.SemaphoreType.DMA],
        compiler_params=pltpu.CompilerParams(vmem_limit_bytes=VMEM_PREPARE),
        cost_estimate=pl.CostEstimate(flops=0, bytes_accessed=8 << 20, transcendentals=0),
        name="prepare",
    )(stiffness, prolongator)
    sent = pl.pallas_call(
        product_kernel,
        out_shape=jax.ShapeDtypeStruct((owners, tiles + 1, PAIR, LANES), jnp.bfloat16),
        in_specs=[smem] * 3 + [vmem] * 6,
        out_specs=vmem,
        scratch_shapes=[
            pltpu.VMEM((row_count + 2 * REACH, width, LANES), jnp.bfloat16),
            pltpu.VMEM((row_count + 2 * REACH, width, LANES), jnp.bfloat16),
            pltpu.VMEM((owners + 1, width, LANES), jnp.float32),
            pltpu.VMEM((owners + 1, width, LANES), jnp.float32),
        ],
        compiler_params=pltpu.CompilerParams(vmem_limit_bytes=VMEM_PRODUCT),
        name="product",
    )(column_index.T, slot_index.T, place_index, a_here, left, right, own_t, first, second)
    received = lax.all_to_all(sent, "rows", 0, 0, tiled=True)
    routed = pl.pallas_call(
        route_kernel,
        out_shape=jax.ShapeDtypeStruct((groups, owners // groups * tiles + 1, PAIR, LANES), jnp.bfloat16),
        in_specs=[vmem],
        out_specs=vmem,
        scratch_shapes=[pltpu.SMEM((groups,), jnp.int32), pltpu.SMEM((owners,), jnp.int32)],
        compiler_params=pltpu.CompilerParams(vmem_limit_bytes=VMEM_SMA392),
        name="route",
    )(received)
    gathered = lax.all_to_all(routed, "sub", 0, 0, tiled=True)
    return pl.pallas_call(
        sum_kernel,
        out_shape=jax.ShapeDtypeStruct((COARSE_DEV, width, width), jnp.float32),
        in_specs=[vmem],
        out_specs=vmem,
        scratch_shapes=[pltpu.VMEM((COARSE_DEV, half, LANES), jnp.float32)],
        compiler_params=pltpu.CompilerParams(vmem_limit_bytes=VMEM_SMA392),
        name="total",
    )(gathered)


def solution(mesh):
    split = ("rows", "sub")
    in_specs = (P(split, None, None), P(split, None, None), P(split, None), P(split, None), P(split, None))
    return jax.shard_map(body, mesh=mesh, in_specs=in_specs, out_specs=P(split, None, None), check_vma=False)
```
